32 devices in a mesh: section: 2 (over x), tensor: 4 (over z), dp: 4 (over y, core).
Axes of the slice: x: 2, y: 2, z: 4, core: 2. Of those that a mesh axis runs over, the one named last changes fastest.
Arguments:
- boundary_in: bfloat16 [2, 4096, 2048], P('section', 'dp'), may hold values from -6 to 6
- segment_ids: int32 [8, 512], P('dp'), may hold values from 0 to 1, never falling along the last dimension, each value on 1 to 312 neighbouring positions
- norm_gains: bfloat16 [2, 2, 2048], P('section'), may hold values from 0.25 to 1.75
- norm_biases: bfloat16 [2, 2, 2048], P('section'), may hold values from -3 to 3
- w_qkv: bfloat16 [2, 2048, 6144], P('section', None, 'tensor'), may hold values from -0.8838835 to 0.8838835, as said below
- b_qkv: bfloat16 [2, 6144], P('section', 'tensor'), may hold values from -3 to 3
- w_out: bfloat16 [2, 2048, 2048], P('section', 'tensor'), may hold values from -0.5 to 0.5
- w_fc: bfloat16 [2, 2048, 8192], P('section', None, 'tensor'), may hold values from -0.125 to 0.125
- b_fc: bfloat16 [2, 8192], P('section', 'tensor'), may hold values from -3 to 3
- w_proj: bfloat16 [2, 8192, 2048], P('section', 'tensor'), may hold values from -0.09375 to 0.09375
- out_biases: bfloat16 [2, 2, 2048], P('section'), may hold values from -2 to 2
Outputs:
- boundary_out: float32 [2, 4096, 2048], P('section', 'dp')
- g_norm_gains: float32 [2, 2, 2048], P('section', None, ('tensor', 'dp'))
- g_norm_biases: float32 [2, 2, 2048], P('section', None, ('tensor', 'dp'))
- g_w_qkv: float32 [2, 2048, 6144], P('section', 'dp', 'tensor')
- g_b_qkv: float32 [2, 6144], P('section', ('tensor', 'dp'))
- g_w_out: float32 [2, 2048, 2048], P('section', 'tensor', 'dp')
- g_w_fc: float32 [2, 2048, 8192], P('section', 'dp', 'tensor')
- g_b_fc: float32 [2, 8192], P('section', ('tensor', 'dp'))
- g_w_proj: float32 [2, 8192, 2048], P('section', 'tensor', 'dp')
- g_out_biases: float32 [2, 2, 2048], P('section', None, 'dp')
The draws below stay inside these ranges and needn't reach their ends.
Inputs may be any that keep to these rules, and one draw needn't show every extreme that they name: `segment_ids`: within each row of 512 tokens the ids never fall and both ids 0 and 1 occur; a document has at most 312 tokens. `w_qkv`: columns come per head in turn as 256 query, 256 key and 256 value columns.
All inputs are finite; a program needn't handle non-finite values.
Results may differ from the reference program's by a relative error of at most 0.013.
Values may be sent and summed in bfloat16 or wider, within the bound.
No kernel may reach another device: no remote copies, remote signals or barrier semaphores. Data moves between devices by JAX's collectives and lax.ppermute only.
A program may use at most 320 MiB of HBM per device.

```python
import math
import jax
import jax.numpy as jnp
import numpy as np
from jax import lax

D = 2048
HEADS = 8
HD = 256
FF = 8192
ROT = 64
SEQ = 512
DOC_MOST = 312
LAYERS = 2
SEQS = 8
TOKENS = 4096


def draw_w_qkv(key, part):
    first_key = jax.random.fold_in(key, 0)
    base = jnp.clip(jax.random.normal(first_key, (LAYERS, D, HEADS, 3, HD), jnp.float32), -6.0, 6.0) * D ** (-0.5)
    return base.reshape(LAYERS, D, 3 * HEADS * HD).astype(jnp.bfloat16)


def spiked(array, key, source, target, shards_of, factor):
    def block_of(dim):
        return (jnp.arange(array.shape[dim]) // (array.shape[dim] // shards_of)).reshape((-1,) + (1,) * (array.ndim - 1 - dim))

    one_side = jax.random.permutation(key, shards_of)[block_of(target)]
    second = (block_of(target) + shards_of // 2) % shards_of
    return jnp.where((block_of(source) == one_side) | (block_of(source) == second), factor * array, array)


def block_scale(rng, dims, cuts, low, high):
    level = 1.0
    for position, blocks in cuts:
        draws = jax.random.uniform(jax.random.fold_in(jax.random.fold_in(rng, 6), position), (blocks,), jnp.float32, low / len(cuts), high / len(cuts))
        level = level * jnp.repeat(jnp.exp(draws), dims[position] // blocks).reshape((-1,) + (1,) * (len(dims) - 1 - position))
    return level


def profile(count, total, most, slope):
    weights = [(1 << 20) // math.isqrt(standing ** slope) + 1 for standing in range(2, count + 1)]
    surplus, given = total - most - (count - 1), [1] * (count - 1)
    while surplus > 0:
        free = [i for i in range(count - 1) if given[i] < most]
        whole, left = sum([weights[i] for i in free]), surplus
        for i in free:
            more = min(most - given[i], max(1, left * weights[i] // whole), surplus)
            given[i] = given[i] + more
            surplus = surplus - more
    return np.array([most] + given)


def uneven(rng, amount, total, reach, slope):
    if amount == 2:
        one = jax.random.randint(rng, (), max(1, total - reach), min(reach, total - 1) + 1)
        return jnp.stack([one, total - one])
    tallies = jnp.asarray(profile(amount, total, reach, slope), jnp.int32)
    couples = (amount - 1) // 2
    source_of, sink = tallies[1:1 + 2 * couples:2], tallies[2:2 + 2 * couples:2]
    slack = jnp.minimum(source_of - 1, reach - sink)
    moved = jax.random.randint(jax.random.fold_in(rng, 1), (couples,), 0, 1 << 20) % (slack + 1)
    tallies = tallies.at[1:1 + 2 * couples:2].set(source_of - moved).at[2:2 + 2 * couples:2].set(sink + moved)
    return tallies[jax.random.permutation(jax.random.fold_in(rng, 2), amount)]


def normal_values(rng, dims, scale, reach, cuts=(), kind=jnp.bfloat16):
    factor_of = block_scale(rng, dims, cuts, -0.22, 0.18) if cuts else 1.0
    values = jax.random.normal(rng, dims, jnp.float32) * scale * factor_of
    return jnp.minimum(jnp.maximum(values, -reach), reach).astype(kind)


def bell_draw_with(stream_key, shape, width, most, cuts, heavy, kind=jnp.bfloat16):
    array = width * jax.random.normal(stream_key, shape, jnp.float32)
    if cuts:
        array = array * block_scale(stream_key, shape, cuts, -0.22, 0.18)
    return jnp.clip(spiked(array, jax.random.fold_in(stream_key, 3), *heavy), -most, most).astype(kind)


def setup_inputs(seed: int = 0) -> dict:
    splits = jax.random.split(jax.random.key(seed), 12)
    boundary_in = bell_draw_with(splits[0], (LAYERS, TOKENS, D), 1.0, 6.0, ((0, 2), (1, 4)), (1, 2, 4, 2.0))
    segment_ids = jax.vmap(lambda own: jnp.searchsorted(jnp.cumsum(uneven(own, 2, SEQ, DOC_MOST, 0)), jnp.arange(SEQ), side="right"))(jax.random.split(splits[1], SEQS)).reshape((SEQS, SEQ)).astype(jnp.int32)
    norm_gains = jnp.clip(1.0 + 0.15 * jax.random.normal(splits[2], (LAYERS, 2, D), jnp.float32), 0.25, 1.75).astype(jnp.bfloat16)
    norm_biases = normal_values(splits[3], (LAYERS, 2, D), 0.5, 3.0, ((0, 2),))
    w_qkv = draw_w_qkv(jax.random.fold_in(splits[11], 71), 0)
    b_qkv = normal_values(splits[5], (LAYERS, 3 * D), 0.5, 3.0, ((0, 2), (1, 4)))
    w_out = normal_values(splits[6], (LAYERS, D, D), (D // 16) ** -0.5, 0.5, ((0, 2), (1, 4)))
    w_fc = normal_values(splits[7], (LAYERS, D, FF), D ** -0.5, 0.125, ((0, 2), (2, 4)))
    b_fc = normal_values(splits[8], (LAYERS, FF), 0.5, 3.0, ((0, 2), (1, 4)))
    w_proj = normal_values(splits[9], (LAYERS, FF, D), (FF // 2) ** -0.5, 0.09375, ((0, 2), (1, 4)))
    out_biases = normal_values(splits[10], (LAYERS, 2, D), 0.3, 2.0, ((0, 2),))
    return {"boundary_in": boundary_in, "segment_ids": segment_ids, "norm_gains": norm_gains, "norm_biases": norm_biases, "w_qkv": w_qkv, "b_qkv": b_qkv, "w_out": w_out, "w_fc": w_fc, "b_fc": b_fc, "w_proj": w_proj, "out_biases": out_biases}


norm_eps = 1e-05
highest = lax.Precision.HIGHEST

@jax.custom_vjp
def low(v):
    return lax.optimization_barrier(v.astype(jnp.bfloat16)).astype(jnp.float32)

@jax.custom_vjp
def low_back(v):
    return v

def low_keep(v):
    return (low(v), None)

def low_pass(kept, grad):
    return (grad,)

def back_keep(v):
    return (v, None)

def back_low(kept, grad):
    return (low(grad),)
low.defvjp(low_keep, low_pass)
low_back.defvjp(back_keep, back_low)

def norm_rows(values, gain, shift):
    center = values - lax.optimization_barrier(jnp.mean(values, axis=-1, keepdims=True))
    spread = lax.optimization_barrier(jnp.mean(center * center, axis=-1, keepdims=True))
    return center * lax.rsqrt(spread + norm_eps) * gain + shift

def rotary_tables(segments):
    places = jnp.arange(segments.shape[0], dtype=jnp.int32)
    starts = jnp.concatenate([jnp.ones((1,), jnp.bool_), segments[1:] != segments[:-1]])
    first_at = lax.cummax(jnp.where(starts, places, 0), axis=0)
    inside = (places - first_at).astype(jnp.float32)
    frequency = 10000.0 ** (-jnp.arange(0, ROT, 2, dtype=jnp.float32) / ROT)
    angles = inside[:, None] * frequency[None, :]
    angles = jnp.concatenate([angles, angles], axis=-1)
    return (jnp.cos(angles), jnp.sin(angles))

def visible(segments):
    places = jnp.arange(segments.shape[0], dtype=jnp.int32)
    return (segments[:, None] == segments[None, :]) & (places[:, None] >= places[None, :])

def rotate(values, cosine, sine):
    half_rot = ROT // 2
    front_part = values[..., :half_rot]
    back_part = values[..., half_rot:ROT]
    turned = jnp.concatenate([-back_part, front_part], axis=-1)
    spun_part = values[..., :ROT] * cosine + turned * sine
    return jnp.concatenate([spun_part, values[..., ROT:]], axis=-1)

def attend(pieces):
    queries, key_rows, value_rows, segments = pieces
    raw_scores = jnp.einsum('qhd,khd->hqk', queries, key_rows, precision=highest) * HD ** (-0.5)
    scores = low_back(raw_scores)
    allowed = visible(segments)
    masked = jnp.where(allowed[None], scores, -1e+30)
    peak_score = lax.optimization_barrier(jnp.max(masked, axis=-1, keepdims=True))
    raised = jnp.exp(masked - peak_score)
    prob_rows = raised / lax.optimization_barrier(jnp.sum(raised, axis=-1, keepdims=True))
    return jnp.einsum('hqk,khd->qhd', low(prob_rows), value_rows, precision=highest)

def layer(inputs, segment_ids, gains, shifts, w_qkv, b_qkv, w_out, w_fc, b_fc, w_proj, out_biases):
    first_norm = low(norm_rows(inputs, gains[0], shifts[0]))
    second_norm = low(norm_rows(inputs, gains[1], shifts[1]))
    mixed_all = low_back(jnp.dot(first_norm, w_qkv, precision=highest) + b_qkv)
    mixed_all = mixed_all.reshape(SEQS, SEQ, HEADS, 3, HD)
    cosine, sine = jax.vmap(rotary_tables)(segment_ids)
    cosine = cosine[:, :, None, :]
    sine = sine[:, :, None, :]
    queries = low(rotate(mixed_all[:, :, :, 0], cosine, sine))
    key_rows = low(rotate(mixed_all[:, :, :, 1], cosine, sine))
    value_rows = low(mixed_all[:, :, :, 2])
    attended = lax.map(jax.checkpoint(attend), (queries, key_rows, value_rows, segment_ids))
    attended = low_back(low(attended.reshape(TOKENS, D)))
    hidden_pre = low_back(jnp.dot(second_norm, w_fc, precision=highest) + b_fc)
    active = low(jax.nn.gelu(hidden_pre, approximate=False))
    branch = low_back(jnp.dot(attended, w_out, precision=highest) + jnp.dot(active, w_proj, precision=highest))
    return inputs + branch + out_biases[0] + out_biases[1]

def reference(boundary_in, segment_ids, norm_gains, norm_biases, w_qkv, b_qkv, w_out, w_fc, b_fc, w_proj, out_biases):
    start = boundary_in[0].astype(jnp.float32)
    cotangent = boundary_in[1].astype(jnp.float32)
    params = tuple((item.astype(jnp.float32) for item in (norm_gains, norm_biases, w_qkv, b_qkv, w_out, w_fc, b_fc, w_proj, out_biases)))

    def forward(inputs, gains, shifts, wqkv_all, bqkv_all, wout_all, wfc_all, bfc_all, wproj_all, outb_all):
        current = inputs
        for level in range(LAYERS):
            if level > 0:
                current = low_back(low(current))
            current = layer(current, segment_ids, gains[level], shifts[level], wqkv_all[level], bqkv_all[level], wout_all[level], wfc_all[level], bfc_all[level], wproj_all[level], outb_all[level])
        return current
    result, pullback = jax.vjp(forward, start, *params)
    grads = pullback(cotangent)
    return (jnp.stack([grads[0], result]), grads[1], grads[2], grads[3], grads[4], grads[5], grads[6], grads[7], grads[8], grads[9])
```

```python
import functools

import jax
import jax.numpy as jnp
from jax import lax
from jax.experimental import pallas as pl
from jax.experimental.pallas import tpu as pltpu
from jax.sharding import PartitionSpec as P

HD = 256
ROT = 64
LANES = 128
QB = 128
EPS = 1e-05
BF = jnp.bfloat16
F32 = jnp.float32


def dot_f32(left, right, dims):
    return lax.dot_general(left, right, (dims, ((), ())), preferred_element_type=F32)


def dot(left, right):
    return dot_f32(left, right, ((1,), (0,)))


def dot_rt(left, right):
    return dot_f32(left, right, ((1,), (1,)))


def dot_lt(left, right):
    return dot_f32(left, right, ((0,), (0,)))


def rotary_tables(segments):
    length = segments.shape[0]
    places = jnp.arange(length, dtype=jnp.int32)
    starts = jnp.concatenate([jnp.ones((1,), jnp.bool_), segments[1:] != segments[:-1]])
    first_at = lax.cummax(jnp.where(starts, places, 0), axis=0)
    inside = (places - first_at).astype(F32)
    frequency = 10000.0 ** (-jnp.arange(0, ROT, 2, dtype=F32) / ROT)
    angles = inside[:, None] * frequency[None, :]
    cosine, sine = jnp.cos(angles), jnp.sin(angles)
    half = ROT // 2
    none = jnp.zeros((length, half), F32)
    rest = jnp.zeros((length, LANES - ROT), F32)
    keep = jnp.concatenate([cosine, cosine, rest + 1.0], axis=1)
    from_right = jnp.concatenate([-sine, none, rest], axis=1)
    from_left = jnp.concatenate([none, sine, rest], axis=1)
    return keep, from_right, from_left


def spin(values, keep, from_right, from_left):
    low, high = values[:, :LANES], values[:, LANES:]
    half = ROT // 2
    turned = (
        low * keep
        + pltpu.roll(low, LANES - half, 1) * from_right
        + pltpu.roll(low, half, 1) * from_left
    )
    return jnp.concatenate([turned, high], axis=1)


def spin_back(grads, keep, from_right, from_left):
    low, high = grads[:, :LANES], grads[:, LANES:]
    half = ROT // 2
    turned = (
        low * keep
        + pltpu.roll(low * from_right, half, 1)
        + pltpu.roll(low * from_left, LANES - half, 1)
    )
    return jnp.concatenate([turned, high], axis=1)


def block_scores(q, k, seg_col, seg_row, at, upto):
    raw = dot_rt(q, k) * HD ** (-0.5)
    rows = lax.broadcasted_iota(jnp.int32, raw.shape, 0) + at
    columns = lax.broadcasted_iota(jnp.int32, raw.shape, 1)
    allowed = (seg_col[at : at + QB] == seg_row[:, :upto]) & (rows >= columns)
    return jnp.where(allowed, raw, -1e30)


def attend_kernel(
    mixed, keep, from_right, from_left, seg_col, seg_row, q_out, k_out, v_out, o_out, lse_out
):
    length = mixed.shape[0]
    tables = (keep[...], from_right[...], from_left[...])
    q_out[...] = spin(mixed[:, :HD], *tables).astype(BF)
    k_out[...] = spin(mixed[:, HD : 2 * HD], *tables).astype(BF)
    v_out[...] = mixed[:, 2 * HD :].astype(BF)
    for at in range(0, length, QB):
        upto = at + QB
        scores = block_scores(
            q_out[at:upto, :], k_out[:upto, :], seg_col, seg_row, at, upto
        )
        peak = jnp.max(scores, axis=-1, keepdims=True)
        raised = jnp.exp(scores - peak)
        total = jnp.sum(raised, axis=-1, keepdims=True)
        probs = (raised / total).astype(BF)
        o_out[at:upto, :] = dot(probs, v_out[:upto, :]).astype(BF)
        lse_out[0, at:upto, :] = peak + jnp.log(total)


def attend(mixed, tables, seg_col, seg_row):
    length, width = mixed.shape
    heads = width // (3 * HD)
    whole = lambda shape: pl.BlockSpec(shape, lambda h: (0, 0))
    by_head = lambda w: pl.BlockSpec((length, w), lambda h: (0, h))
    flat = jax.ShapeDtypeStruct((length, heads * HD), BF)
    pairs = heads * length * (length + QB) // 2
    return pl.pallas_call(
        attend_kernel,
        grid=(heads,),
        in_specs=[by_head(3 * HD)]
        + [whole((length, LANES))] * 3
        + [whole((length, 1)), whole((1, length))],
        out_specs=[by_head(HD)] * 4 + [pl.BlockSpec((1, length, 1), lambda h: (h, 0, 0))],
        out_shape=[flat] * 4 + [jax.ShapeDtypeStruct((heads, length, 1), F32)],
        cost_estimate=pl.CostEstimate(
            flops=4 * pairs * HD,
            bytes_accessed=length * width * 4 + 8 * length * heads * HD,
            transcendentals=pairs,
        ),
        name="attend",
    )(mixed, *tables, seg_col, seg_row)


def attend_back_kernel(
    q, k, v, d_o, lse, keep, from_right, from_left, seg_col, seg_row, d_out, sum_out, dk_acc, dv_acc
):
    length = q.shape[0]
    dk_acc[...] = jnp.zeros_like(dk_acc)
    dv_acc[...] = jnp.zeros_like(dv_acc)
    tables = (keep[...], from_right[...], from_left[...])
    total_q = jnp.zeros((1, HD), F32)
    for at in range(0, length, QB):
        upto = at + QB
        q_now, d_now = q[at:upto, :], d_o[at:upto, :]
        scores = block_scores(q_now, k[:upto, :], seg_col, seg_row, at, upto)
        probs = jnp.exp(scores - lse[0, at:upto, :])
        d_probs = dot_rt(d_now, v[:upto, :])
        row = jnp.sum(probs * d_probs, axis=-1, keepdims=True)
        d_scores = (probs * (d_probs - row)).astype(BF)
        dq = dot(d_scores, k[:upto, :]) * HD ** (-0.5)
        dq = spin_back(dq, *(t[at:upto] for t in tables)).astype(BF)
        d_out[at:upto, :HD] = dq
        total_q += jnp.sum(dq.astype(F32), axis=0, keepdims=True)
        dk_acc[:upto, :] += dot_lt(d_scores, q_now)
        dv_acc[:upto, :] += dot_lt(probs.astype(BF), d_now)
    dk = spin_back(dk_acc[...] * HD ** (-0.5), *tables).astype(BF)
    d_out[:, HD : 2 * HD] = dk
    dv = dv_acc[...].astype(BF)
    d_out[:, 2 * HD :] = dv
    sum_out[:, :HD] = total_q
    sum_out[:, HD : 2 * HD] = jnp.sum(dk.astype(F32), axis=0, keepdims=True)
    sum_out[:, 2 * HD :] = jnp.sum(dv.astype(F32), axis=0, keepdims=True)


def attend_back(q, k, v, d_o, lse, tables, seg_col, seg_row):
    length, width = q.shape
    heads = width // HD
    whole = lambda shape: pl.BlockSpec(shape, lambda h: (0, 0))
    by_head = lambda rows, w: pl.BlockSpec((rows, w), lambda h: (0, h))
    pairs = heads * length * (length + QB) // 2
    return pl.pallas_call(
        attend_back_kernel,
        grid=(heads,),
        in_specs=[by_head(length, HD)] * 4
        + [pl.BlockSpec((1, length, 1), lambda h: (h, 0, 0))]
        + [whole((length, LANES))] * 3
        + [whole((length, 1)), whole((1, length))],
        out_specs=[by_head(length, 3 * HD), by_head(1, 3 * HD)],
        out_shape=[
            jax.ShapeDtypeStruct((length, 3 * width), BF),
            jax.ShapeDtypeStruct((1, 3 * width), F32),
        ],
        scratch_shapes=[pltpu.VMEM((length, HD), F32)] * 2,
        cost_estimate=pl.CostEstimate(
            flops=10 * pairs * HD,
            bytes_accessed=14 * length * width,
            transcendentals=pairs,
        ),
        name="attend_back",
    )(q, k, v, d_o, lse, *tables, seg_col, seg_row)


def row_stats(values):
    center = values - jnp.mean(values, axis=-1, keepdims=True)
    spread = jnp.mean(center * center, axis=-1, keepdims=True)
    inverse = lax.rsqrt(spread + EPS)
    return center * inverse, inverse


def norm_back(grads, hat, inverse):
    return (
        grads
        - jnp.mean(grads, axis=-1, keepdims=True)
        - hat * jnp.mean(grads * hat, axis=-1, keepdims=True)
    ) * inverse


def own_block(values, at, count):
    size = values.shape[0] // count
    return lax.dynamic_slice_in_dim(values, at * size, size, 0)


def scatter_rows(partial, axis, count, at):
    pieces = [own_block(partial, at, count)]
    for step in range(1, count):
        route = [(i, (i + step) % count) for i in range(count)]
        block = own_block(partial, (at + step) % count, count)
        pieces.append(lax.ppermute(block, axis, route))
    return functools.reduce(jnp.add, [piece.astype(F32) for piece in pieces])


def gather_rows(block, count, at, send):
    size = block.shape[0]
    whole = jnp.zeros((count * size,) + block.shape[1:], block.dtype)
    for step in range(count):
        whole = lax.dynamic_update_slice_in_dim(
            whole, send(block, step), ((at - step) % count) * size, 0
        )
    return whole


def shards(
    boundary_in,
    segment_ids,
    norm_gains,
    norm_biases,
    w_qkv,
    b_qkv,
    w_out,
    w_fc,
    b_fc,
    w_proj,
    out_biases,
):
    w_qkv, w_out, w_fc, w_proj = w_qkv[0], w_out[0], w_fc[0], w_proj[0]
    b_qkv, b_fc = b_qkv[0].astype(F32), b_fc[0].astype(F32)
    gains, shifts = norm_gains[0].astype(F32), norm_biases[0].astype(F32)
    added = out_biases[0, 0].astype(F32) + out_biases[0, 1].astype(F32)
    seqs, length = segment_ids.shape
    width = boundary_in.shape[2]
    ends = [boundary_in[0, s * length : (s + 1) * length] for s in range(seqs)]
    section = lax.axis_index("section")
    lane = lax.axis_index("tensor")
    count = lax.axis_size("tensor")
    first = section == 0

    tables = [rotary_tables(segment_ids[s]) for s in range(seqs)]
    columns = [segment_ids[s][:, None] for s in range(seqs)]
    lines = [segment_ids[s][None, :] for s in range(seqs)]

    def across(origin):
        def send(block, step):
            target = 1 - origin
            route = [
                (origin * count + i, target * count + (i + step) % count) for i in range(count)
            ]
            return lax.ppermute(block, ("section", "tensor"), route)

        return send

    def within(block, step):
        if step == 0:
            return block
        return lax.ppermute(block, "tensor", [(i, (i + step) % count) for i in range(count)])

    def forward(rows, s):
        hat, _ = row_stats(rows.astype(F32))
        n1 = (hat * gains[0] + shifts[0]).astype(BF)
        n2 = (hat * gains[1] + shifts[1]).astype(BF)
        mixed = dot(n1, w_qkv) + b_qkv
        q, k, v, o, lse = attend(mixed, tables[s], columns[s], lines[s])
        u = dot(n2, w_fc) + b_fc
        half_erf = 0.5 * (1.0 + lax.erf(u * 0.7071067811865476))
        a = (u * half_erf).astype(BF)
        slope = (half_erf + u * jnp.exp(-0.5 * u * u) * 0.3989422804014327).astype(BF)
        partial = (dot(o, w_out) + dot(a, w_proj)).astype(BF)
        return partial, (rows, n1, n2, q, k, v, o, lse, a, slope)

    def backward(kept, dyb, s):
        rows, n1, n2, q, k, v, o, lse, a, slope = kept
        d_u = (dot_rt(dyb, w_proj) * slope.astype(F32)).astype(BF)
        d_o = dot_rt(dyb, w_out).astype(BF)
        d_mixed, d_bqkv = attend_back(q, k, v, d_o, lse, tables[s], columns[s], lines[s])
        d_n1 = dot_rt(d_mixed, w_qkv)
        d_n2 = dot_rt(d_u, w_fc)
        error = (d_n1 * gains[0] + d_n2 * gains[1]).astype(BF)
        hat, _ = row_stats(rows.astype(F32))
        d_gain = jnp.stack([jnp.sum(d_n1 * hat, axis=0), jnp.sum(d_n2 * hat, axis=0)])
        d_shift = jnp.stack([jnp.sum(d_n1, axis=0), jnp.sum(d_n2, axis=0)])
        d_bfc = jnp.sum(d_u.astype(F32), axis=0)
        d_outb = jnp.sum(dyb.astype(F32), axis=0)
        small = (d_gain, d_shift, d_bqkv[0], d_bfc, d_outb)
        return error, (n1, n2, o, a, dyb, d_u, d_mixed), small

    def weight_grads(left):
        n1, n2, o, a, dyb, d_u, d_mixed = (jnp.concatenate(item, 0) for item in zip(*left))
        return (
            dot_lt(n1, d_mixed).astype(BF),
            dot_lt(o, dyb).astype(BF),
            dot_lt(n2, d_u).astype(BF),
            dot_lt(a, dyb).astype(BF),
        )

    def input_grad(total, rows, dyb):
        hat, inverse = row_stats(rows.astype(F32))
        return norm_back(total, hat, inverse) + dyb.astype(F32)

    early, sums = [], []
    for s in range(seqs):
        partial, kept = forward(ends[s], s)
        early.append(kept)
        sums.append(scatter_rows(partial, "tensor", count, lane))
    inputs = []
    for s in range(seqs):
        own = own_block(ends[s], lane, count).astype(F32) + sums[s] + added
        inputs.append(gather_rows(own.astype(BF), count, lane, across(0)))

    late_out, late, small_late, returning = [], [], [], []
    for s in range(seqs):
        partial, kept = forward(inputs[s], s)
        late_out.append(partial)
        error, left, small = backward(kept, ends[s], s)
        late.append(left)
        small_late.append(small)
        total = scatter_rows(error, "tensor", count, lane)
        own = input_grad(
            total, own_block(inputs[s], lane, count), own_block(ends[s], lane, count)
        )
        returning.append(gather_rows(own.astype(BF), count, lane, across(1)))
    grads_late = weight_grads(late)

    left_early, small_early, results = [], [], []
    for s in range(seqs):
        error, left, small = backward(early[s], returning[s], s)
        left_early.append(left)
        small_early.append(small)
        final = jnp.where(first, error, late_out[s])
        total = scatter_rows(final, "tensor", count, lane)
        own_end = own_block(ends[s], lane, count)
        own_in = input_grad(total, own_end, own_block(returning[s], lane, count))
        own_out = own_block(inputs[s], lane, count).astype(F32) + total + added
        own = jnp.where(first, own_in, own_out).astype(BF)
        results.append(gather_rows(own, count, lane, within))
    grads_early = weight_grads(left_early)

    boundary_out = jnp.concatenate(results, 0).astype(F32)[None]
    grads = [jnp.where(first, x, y) for x, y in zip(grads_early, grads_late)]
    small = [
        jnp.where(first, functools.reduce(jnp.add, x), functools.reduce(jnp.add, y))
        for x, y in zip(zip(*small_early), zip(*small_late))
    ]
    d_gain, d_shift, d_bqkv, d_bfc, d_outb = small

    def over_dp(values, dim):
        return lax.psum_scatter(values, "dp", scatter_dimension=dim, tiled=True).astype(F32)

    both = ("tensor", "dp")
    g_qkv, g_out, g_fc, g_proj = grads
    g_outb = over_dp(d_outb[None], 1)
    return (
        boundary_out,
        lax.psum_scatter(d_gain, both, scatter_dimension=1, tiled=True)[None],
        lax.psum_scatter(d_shift, both, scatter_dimension=1, tiled=True)[None],
        over_dp(g_qkv, 0)[None],
        over_dp(d_bqkv, 0)[None],
        over_dp(g_out, 1)[None],
        over_dp(g_fc, 0)[None],
        over_dp(d_bfc, 0)[None],
        over_dp(g_proj, 1)[None],
        jnp.concatenate([g_outb, g_outb], 0)[None],
    )


def solution(mesh):
    return jax.shard_map(
        shards,
        mesh=mesh,
        in_specs=(
            P("section", "dp", None),
            P("dp", None),
            P("section", None, None),
            P("section", None, None),
            P("section", None, "tensor"),
            P("section", "tensor"),
            P("section", "tensor", None),
            P("section", None, "tensor"),
            P("section", "tensor"),
            P("section", "tensor", None),
            P("section", None, None),
        ),
        out_specs=(
            P("section", "dp", None),
            P("section", None, ("tensor", "dp")),
            P("section", None, ("tensor", "dp")),
            P("section", "dp", "tensor"),
            P("section", ("tensor", "dp")),
            P("section", "tensor", "dp"),
            P("section", "dp", "tensor"),
            P("section", ("tensor", "dp")),
            P("section", "tensor", "dp"),
            P("section", None, "dp"),
        ),
        check_vma=False,
    )
```

```python
import functools

import jax
import jax.numpy as jnp
from jax import lax
from jax.experimental import pallas as pl
from jax.experimental.pallas import tpu as pltpu
from jax.sharding import PartitionSpec as P

HD = 256
ROT = 64
LANES = 128
QB = 256
FT = 512
RB = 128
EPS = 1e-05
BF = jnp.bfloat16
F32 = jnp.float32


def dot_f32(left, right, dims):
    return lax.dot_general(left, right, (dims, ((), ())), preferred_element_type=F32)


def dot(left, right):
    return dot_f32(left, right, ((1,), (0,)))


def dot_rt(left, right):
    return dot_f32(left, right, ((1,), (1,)))


def dot_lt(left, right):
    return dot_f32(left, right, ((0,), (0,)))


def rotary_tables(segments):
    length = segments.shape[0]
    places = jnp.arange(length, dtype=jnp.int32)
    starts = jnp.concatenate([jnp.ones((1,), jnp.bool_), segments[1:] != segments[:-1]])
    first_at = lax.cummax(jnp.where(starts, places, 0), axis=0)
    inside = (places - first_at).astype(F32)
    frequency = 10000.0 ** (-jnp.arange(0, ROT, 2, dtype=F32) / ROT)
    angles = inside[:, None] * frequency[None, :]
    cosine, sine = jnp.cos(angles), jnp.sin(angles)
    half = ROT // 2
    none = jnp.zeros((length, half), F32)
    rest = jnp.zeros((length, LANES - ROT), F32)
    keep = jnp.concatenate([cosine, cosine, rest + 1.0], axis=1)
    from_right = jnp.concatenate([-sine, none, rest], axis=1)
    from_left = jnp.concatenate([none, sine, rest], axis=1)
    return keep, from_right, from_left


def spin(values, keep, from_right, from_left):
    low, high = values[:, :LANES], values[:, LANES:]
    half = ROT // 2
    turned = (
        low * keep
        + pltpu.roll(low, LANES - half, 1) * from_right
        + pltpu.roll(low, half, 1) * from_left
    )
    return jnp.concatenate([turned, high], axis=1)


def spin_back(grads, keep, from_right, from_left):
    low, high = grads[:, :LANES], grads[:, LANES:]
    half = ROT // 2
    turned = (
        low * keep
        + pltpu.roll(low * from_right, half, 1)
        + pltpu.roll(low * from_left, LANES - half, 1)
    )
    return jnp.concatenate([turned, high], axis=1)


def block_scores(q, k, seg_col, seg_row, at, upto):
    raw = dot_rt(q, k) * HD ** (-0.5)
    rows = lax.broadcasted_iota(jnp.int32, raw.shape, 0) + at
    columns = lax.broadcasted_iota(jnp.int32, raw.shape, 1)
    allowed = (seg_col[at:upto] == seg_row[:, :upto]) & (rows >= columns)
    return jnp.where(allowed, raw, -1e30)


def row_stats(values):
    center = values - jnp.mean(values, axis=-1, keepdims=True)
    spread = jnp.mean(center * center, axis=-1, keepdims=True)
    inverse = lax.rsqrt(spread + EPS)
    return center * inverse, inverse


def row_blocks(length):
    return [(at, min(at + RB, length)) for at in range(0, length, RB)]


def forward_kernel(heads, with_pulled, *refs):
    (
        rows, gains, shifts, w_qkv, b_qkv, keep, from_right, from_left, seg_col, seg_row,
        w_out, w_fc, b_fc, w_proj,
    ) = refs[:14]
    refs = refs[14:]
    if with_pulled:
        pulled, refs = refs[0], refs[1:]
    n1, n2, q_out, k_out, v_out, o_out, lse_out, a_out, side_out, partial, total = refs
    step = pl.program_id(0)
    length = rows.shape[0]

    @pl.when(step == 0)
    def _():
        for at, to in row_blocks(length):
            hat, _ = row_stats(rows[at:to, :].astype(F32))
            n1[at:to, :] = (hat * gains[0:1, :] + shifts[0:1, :]).astype(BF)
            n2[at:to, :] = (hat * gains[1:2, :] + shifts[1:2, :]).astype(BF)

    @pl.when(step < heads)
    def _():
        tables = (keep[...], from_right[...], from_left[...])
        mixed = dot(n1[...], w_qkv[...]) + b_qkv[...]
        q_out[...] = spin(mixed[:, :HD], *tables).astype(BF)
        k_out[...] = spin(mixed[:, HD : 2 * HD], *tables).astype(BF)
        v_out[...] = mixed[:, 2 * HD :].astype(BF)
        for at in range(0, length, QB):
            upto = at + QB
            scores = block_scores(
                q_out[at:upto, :], k_out[:upto, :], seg_col, seg_row, at, upto
            )
            peak = jnp.max(scores, axis=-1, keepdims=True)
            raised = jnp.exp(scores - peak)
            weight = jnp.sum(raised, axis=-1, keepdims=True)
            probs = (raised / weight).astype(BF)
            o_out[at:upto, :] = dot(probs, v_out[:upto, :]).astype(BF)
            lse_out[0, at:upto, :] = peak + jnp.log(weight)
        part = dot(o_out[...], w_out[...])

        @pl.when(step == 0)
        def _():
            total[...] = part

        @pl.when(step > 0)
        def _():
            total[...] += part

    @pl.when(step >= heads)
    def _():
        for at, to in row_blocks(length):
            u = dot(n2[at:to, :], w_fc[...]) + b_fc[...]
            half_erf = 0.5 * (1.0 + lax.erf(u * 0.7071067811865476))
            a = (u * half_erf).astype(BF)
            slope = half_erf + u * jnp.exp(-0.5 * u * u) * 0.3989422804014327
            if with_pulled:
                slope = slope * pulled[at:to, :].astype(F32)
            a_out[at:to, :] = a
            side_out[at:to, :] = slope.astype(BF)
            total[at:to, :] += dot(a, w_proj[...])

    @pl.when(step == pl.num_programs(0) - 1)
    def _():
        partial[...] = total[...].astype(BF)


def fixed(shape):
    return pl.BlockSpec(shape, lambda i: (0,) * len(shape))


def forward_pass(rows, tables, seg_col, seg_row, weights, pulled):
    gains, shifts, w_qkv, b_qkv, w_out, w_fc, b_fc, w_proj = weights
    length, width = rows.shape
    heads = w_out.shape[0] // HD
    hidden = w_fc.shape[1]
    tiles = hidden // FT
    head = lambda i: jnp.minimum(i, heads - 1)
    tile = lambda i: jnp.maximum(i - heads, 0)
    by_head = lambda r, c: pl.BlockSpec((r, c), lambda i: (0, head(i)))
    by_tile = lambda r, c: pl.BlockSpec((r, c), lambda i: (0, tile(i)))
    shape = jax.ShapeDtypeStruct
    operands = [
        rows, gains, shifts, w_qkv, b_qkv[None], *tables, seg_col, seg_row, w_out, w_fc,
        b_fc[None], w_proj,
    ]
    in_specs = [
        fixed((length, width)),
        fixed((2, width)),
        fixed((2, width)),
        by_head(width, 3 * HD),
        by_head(1, 3 * HD),
        *[fixed((length, LANES))] * 3,
        fixed((length, 1)),
        fixed((1, length)),
        pl.BlockSpec((HD, width), lambda i: (head(i), 0)),
        by_tile(width, FT),
        by_tile(1, FT),
        pl.BlockSpec((FT, width), lambda i: (tile(i), 0)),
    ]
    if pulled is not None:
        operands.append(pulled)
        in_specs.append(by_tile(length, FT))
    flops = 2 * length * width * (4 * heads * HD + 2 * hidden)
    return pl.pallas_call(
        functools.partial(forward_kernel, heads, pulled is not None),
        grid=(heads + tiles,),
        in_specs=in_specs,
        out_specs=[
            fixed((length, width)),
            fixed((length, width)),
            *[by_head(length, HD)] * 4,
            pl.BlockSpec((1, length, 1), lambda i: (head(i), 0, 0)),
            by_tile(length, FT),
            by_tile(length, FT),
            fixed((length, width)),
        ],
        out_shape=[
            shape((length, width), BF),
            shape((length, width), BF),
            *[shape((length, heads * HD), BF)] * 4,
            shape((heads, length, 1), F32),
            shape((length, hidden), BF),
            shape((length, hidden), BF),
            shape((length, width), BF),
        ],
        scratch_shapes=[pltpu.VMEM((length, width), F32)],
        cost_estimate=pl.CostEstimate(
            flops=flops, bytes_accessed=2 * width * (4 * heads * HD + 2 * hidden), transcendentals=0
        ),
        compiler_params=pltpu.CompilerParams(vmem_limit_bytes=60 << 20),
    )(*operands)


def backward_kernel(heads, ready, *refs):
    (
        rows, gains, q, k, v, lse, keep, from_right, from_left, seg_col, seg_row, w_qkv,
        side, w_fc,
    ) = refs[:14]
    refs = refs[14:]
    if ready:
        d_o, refs = refs[0], refs[1:]
        error, d_mixed, sums, d_bqkv, d_bfc, one, two, dk_acc, dv_acc = refs
        d_u = None
    else:
        (
            dyb, w_out, w_proj, error, d_mixed, sums, d_bqkv, d_bfc, d_u, one, two,
            dk_acc, dv_acc,
        ) = refs
    step = pl.program_id(0)
    length = rows.shape[0]
    scale = HD ** (-0.5)

    @pl.when(step < heads)
    def _():
        tables = (keep[...], from_right[...], from_left[...])
        total_q = jnp.zeros((1, HD), F32)
        out = d_o[...] if ready else dot_rt(dyb[...], w_out[...]).astype(BF)
        dk_acc[...] = jnp.zeros_like(dk_acc)
        dv_acc[...] = jnp.zeros_like(dv_acc)
        for at in range(0, length, QB):
            upto = at + QB
            q_now, d_now = q[at:upto, :], out[at:upto]
            scores = block_scores(q_now, k[:upto, :], seg_col, seg_row, at, upto)
            probs = jnp.exp(scores - lse[0, at:upto, :])
            d_probs = dot_rt(d_now, v[:upto, :])
            row = jnp.sum(probs * d_probs, axis=-1, keepdims=True)
            d_scores = (probs * (d_probs - row)).astype(BF)
            dq = dot(d_scores, k[:upto, :]) * scale
            dq = spin_back(dq, *(t[at:upto] for t in tables)).astype(BF)
            d_mixed[at:upto, :HD] = dq
            total_q += jnp.sum(dq.astype(F32), axis=0, keepdims=True)
            dk_acc[:upto, :] += dot_lt(d_scores, q_now)
            dv_acc[:upto, :] += dot_lt(probs.astype(BF), d_now)
        dk = spin_back(dk_acc[...] * scale, *tables).astype(BF)
        d_mixed[:, HD : 2 * HD] = dk
        dv = dv_acc[...].astype(BF)
        d_mixed[:, 2 * HD :] = dv
        d_bqkv[:, :HD] = total_q
        d_bqkv[:, HD : 2 * HD] = jnp.sum(dk.astype(F32), axis=0, keepdims=True)
        d_bqkv[:, 2 * HD :] = jnp.sum(dv.astype(F32), axis=0, keepdims=True)
        part = dot_rt(d_mixed[...], w_qkv[...])

        @pl.when(step == 0)
        def _():
            one[...] = part
            two[...] = jnp.zeros_like(two)

        @pl.when(step > 0)
        def _():
            one[...] += part

    @pl.when(step >= heads)
    def _():
        bias = jnp.zeros(d_bfc.shape, F32)
        for at, to in row_blocks(length):
            if ready:
                d_now = side[at:to, :]
            else:
                d_now = dot_rt(dyb[at:to, :], w_proj[...]) * side[at:to, :].astype(F32)
                d_now = d_now.astype(BF)
                d_u[at:to, :] = d_now
            bias += jnp.sum(d_now.astype(F32), axis=0, keepdims=True)
            two[at:to, :] += dot_rt(d_now, w_fc[...])
        d_bfc[...] = bias

    @pl.when(step == pl.num_programs(0) - 1)
    def _():
        found = [jnp.zeros((1, rows.shape[1]), F32) for _ in range(4)]
        for at, to in row_blocks(length):
            hat, inverse = row_stats(rows[at:to, :].astype(F32))
            first, second = one[at:to, :], two[at:to, :]
            for i, term in enumerate((first * hat, second * hat, first, second)):
                found[i] += jnp.sum(term, axis=0, keepdims=True)
            both = first * gains[0:1, :] + second * gains[1:2, :]
            both = (
                both
                - jnp.mean(both, axis=-1, keepdims=True)
                - hat * jnp.mean(both * hat, axis=-1, keepdims=True)
            ) * inverse
            error[at:to, :] = both.astype(BF)
        for i in range(4):
            sums[i : i + 1, :] = found[i]


def backward_pass(kept, dyb, d_o, tables, seg_col, seg_row, weights):
    gains, _, w_qkv, _, w_out, w_fc, _, w_proj = weights
    rows, n1, n2, q, k, v, o, lse, a, side = kept
    ready = d_o is not None
    length, width = rows.shape
    heads = w_out.shape[0] // HD
    hidden = w_fc.shape[1]
    tiles = hidden // FT
    head = lambda i: jnp.minimum(i, heads - 1)
    tile = lambda i: jnp.maximum(i - heads, 0)
    by_head = lambda r, c: pl.BlockSpec((r, c), lambda i: (0, head(i)))
    by_tile = lambda r, c: pl.BlockSpec((r, c), lambda i: (0, tile(i)))
    shape = jax.ShapeDtypeStruct
    operands = [rows, gains, q, k, v, lse, *tables, seg_col, seg_row, w_qkv, side, w_fc]
    in_specs = [
        fixed((length, width)),
        fixed((2, width)),
        *[by_head(length, HD)] * 3,
        pl.BlockSpec((1, length, 1), lambda i: (head(i), 0, 0)),
        *[fixed((length, LANES))] * 3,
        fixed((length, 1)),
        fixed((1, length)),
        by_head(width, 3 * HD),
        by_tile(length, FT),
        by_tile(width, FT),
    ]
    out_specs = [
        fixed((length, width)),
        by_head(length, 3 * HD),
        fixed((4, width)),
        by_head(1, 3 * HD),
        by_tile(1, FT),
    ]
    out_shape = [
        shape((length, width), BF),
        shape((length, 3 * heads * HD), BF),
        shape((4, width), F32),
        shape((1, 3 * heads * HD), F32),
        shape((1, hidden), F32),
    ]
    if ready:
        operands.append(d_o)
        in_specs.append(by_head(length, HD))
    else:
        operands += [dyb, w_out, w_proj]
        in_specs += [
            fixed((length, width)),
            pl.BlockSpec((HD, width), lambda i: (head(i), 0)),
            pl.BlockSpec((FT, width), lambda i: (tile(i), 0)),
        ]
        out_specs.append(by_tile(length, FT))
        out_shape.append(shape((length, hidden), BF))
    flops = 2 * length * width * (3 * heads * HD + hidden) * (1 if ready else 2)
    result = pl.pallas_call(
        functools.partial(backward_kernel, heads, ready),
        grid=(heads + tiles,),
        in_specs=in_specs,
        out_specs=out_specs,
        out_shape=out_shape,
        scratch_shapes=[pltpu.VMEM((length, width), F32)] * 2
        + [pltpu.VMEM((length, HD), F32)] * 2,
        cost_estimate=pl.CostEstimate(
            flops=flops, bytes_accessed=2 * width * (3 * heads * HD + hidden), transcendentals=0
        ),
        compiler_params=pltpu.CompilerParams(vmem_limit_bytes=60 << 20),
    )(*operands)
    if ready:
        result = [*result, side]
    error, d_mixed, sums, d_bqkv, d_bfc, d_u = result
    return error, (n1, n2, o, a, dyb, d_u, d_mixed), (sums, d_bqkv[0], d_bfc[0])


def own_block(values, at, count):
    size = values.shape[0] // count
    return lax.dynamic_slice_in_dim(values, at * size, size, 0)


def tie(values, *earlier):
    return lax.optimization_barrier((values, earlier))[0]


def shards(
    boundary_in,
    segment_ids,
    norm_gains,
    norm_biases,
    w_qkv,
    b_qkv,
    w_out,
    w_fc,
    b_fc,
    w_proj,
    out_biases,
):
    w_qkv, w_out, w_fc, w_proj = w_qkv[0], w_out[0], w_fc[0], w_proj[0]
    b_qkv, b_fc = b_qkv[0].astype(F32), b_fc[0].astype(F32)
    gains, shifts = norm_gains[0].astype(F32), norm_biases[0].astype(F32)
    added = out_biases[0, 0].astype(F32) + out_biases[0, 1].astype(F32)
    weights = (gains, shifts, w_qkv, b_qkv, w_out, w_fc, b_fc, w_proj)
    seqs, length = segment_ids.shape
    ends = [boundary_in[0, s * length : (s + 1) * length] for s in range(seqs)]
    section = lax.axis_index("section")
    lane = lax.axis_index("tensor")
    count = lax.axis_size("tensor")
    first = section == 0
    dp = lax.axis_index("dp")
    dp_count = lax.axis_size("dp")

    tables = [rotary_tables(segment_ids[s]) for s in range(seqs)]
    columns = [segment_ids[s][:, None] for s in range(seqs)]
    lines = [segment_ids[s][None, :] for s in range(seqs)]

    def own(values):
        return own_block(values, lane, count)

    def ring(step, origin, target):
        return [(origin * count + i, target * count + (i + step) % count) for i in range(count)]

    both = ("section", "tensor")

    def scatter(partial, addend, origin):
        pieces = []
        for step in range(count):
            block = own_block(partial, (lane + step) % count, count)
            if step == 0:
                block = (block.astype(F32) + addend).astype(BF)
            pieces.append(lax.ppermute(block, both, ring(step, origin, 1 - origin)))
        return pieces

    def scatter_within(partial, addend):
        pieces = [own(partial).astype(F32) + addend]
        for step in range(1, count):
            block = own_block(partial, (lane + step) % count, count)
            route = [(i, (i + step) % count) for i in range(count)]
            pieces.append(lax.ppermute(block, "tensor", route))
        return pieces

    def summed(pieces):
        return functools.reduce(jnp.add, [p.astype(F32) for p in pieces]).astype(BF)

    def gather(block, where=None):
        size = block.shape[0]
        whole = jnp.zeros((count * size,) + block.shape[1:], block.dtype)
        for step in range(count):
            piece = block
            if step:
                if where is None:
                    route = [(i, (i + step) % count) for i in range(count)]
                    piece = lax.ppermute(block, "tensor", route)
                else:
                    piece = lax.ppermute(block, both, ring(step, where, where))
            whole = lax.dynamic_update_slice_in_dim(
                whole, piece, ((lane - step) % count) * size, 0
            )
        return whole

    def pull_back(dyb):
        return dot_rt(dyb, w_proj).astype(BF), dot_rt(dyb, w_out).astype(BF)

    def forward(rows, s, pulled=None):
        result = forward_pass(rows, tables[s], columns[s], lines[s], weights, pulled)
        return result[-1], (rows, *result[:-1])

    def backward(kept, dyb, d_o, s):
        return backward_pass(kept, dyb, d_o, tables[s], columns[s], lines[s], weights)

    def joined(left):
        return [jnp.concatenate(item, 0) for item in zip(*left)]

    def grad_block(which, joint, block):
        n1, n2, o, a, dyb, d_u, d_mixed = joint
        left, right, cut_left = (
            (a, dyb, False),
            (o, dyb, False),
            (n2, d_u, True),
            (n1, d_mixed, True),
        )[which]
        cut = left if cut_left else right
        size = cut.shape[1] // dp_count
        piece = lax.dynamic_slice_in_dim(cut, block * size, size, 1)
        return dot_lt(piece, right) if cut_left else dot_lt(left, piece)

    half_dp = dp_count // 2
    group, core = dp // 2, dp % 2
    away = [((group + g) % half_dp) * 2 + 1 - core for g in range(half_dp)]
    near = [((group + g) % half_dp) * 2 + core for g in range(half_dp)]

    def to_core(values):
        return lax.ppermute(values, "dp", [(i, i ^ 1) for i in range(dp_count)])

    def to_group(values, step):
        route = [(i, (i + 2 * step) % dp_count) for i in range(dp_count)]
        return lax.ppermute(values, "dp", route)

    early, pieces, partial = [], [], None
    for s in range(seqs):
        rows = ends[s] if s == 0 else tie(ends[s], partial)
        partial, kept = forward(rows, s)
        early.append(kept)
        addend = tie(own(ends[s]).astype(F32) + added, partial)
        pieces.append(scatter(partial, addend, 0))
    pulled = []
    for s in range(seqs):
        pulled.append(pull_back(tie(ends[s], partial, *pulled)))
    blocks = []
    for s in range(seqs):
        pieces[s][0] = tie(pieces[s][0], pulled, *blocks)
        blocks.append(summed(pieces[s]))
    inputs = [gather(block, 1) for block in blocks]
    inputs[0] = tie(inputs[0], blocks[-1])

    late_out, late, small_late, error, pieces = [], [], [], None, []
    for s in range(seqs):
        rows = inputs[s] if s == 0 else tie(inputs[s], error)
        partial, kept = forward(rows, s, pulled[s][0])
        late_out.append(partial)
        d_o = tie(pulled[s][1], partial)
        error, left, small = backward(kept, ends[s], d_o, s)
        late.append(left)
        small_late.append(small)
        pieces.append(scatter(error, tie(own(ends[s]), error).astype(F32), 1))
    pieces[0][0] = tie(pieces[0][0], error)
    blocks = [summed(pieces[0])]
    joint = joined(tie(late, blocks[-1]))

    def late_grads(joint, chosen):
        found = {}
        for which, b, index in chosen:
            found[index] = grad_block(which, joint, b).astype(BF)
            joint = tie(joint, found[index])
        return found, joint

    jobs = [(w, b, (w, "away", g)) for w in range(4) for g, b in enumerate(away)]
    jobs += [(w, b, (w, "near", g)) for w in range(4) for g, b in enumerate(near)]
    split = 3 * len(jobs) // 4
    grads_late, joint = late_grads(joint, jobs[:split])
    for s in range(1, seqs):
        pieces[s][0] = tie(pieces[s][0], joint, *blocks)
        blocks.append(summed(pieces[s]))
    more, joint = late_grads(tie(joint, blocks[-1]), jobs[split:])
    grads_late.update(more)
    returning = [gather(block, 0) for block in blocks]

    left_early, small_early, pieces, earlier = [], [], [], joint
    for s in range(seqs):
        dyb = tie(returning[s], earlier)
        error, left, small = backward(early[s], dyb, None, s)
        left_early.append(left)
        small_early.append(small)
        final = jnp.where(first, error, late_out[s])
        addend = jnp.where(
            first,
            own(returning[s]).astype(F32),
            own(inputs[s]).astype(F32) + added,
        )
        pieces.append(scatter_within(final, addend))
        earlier = final
    joint = joined(tie(left_early, earlier))

    def chosen(which, block, kept):
        return jnp.where(first, grad_block(which, joint, block), kept.astype(F32))

    arrived = []
    for w in range(4):
        sent = jnp.stack(
            [
                chosen(w, b, grads_late[w, "away", g]).astype(BF)
                for g, b in enumerate(away)
            ]
        )
        arrived.append(to_core(sent))
        joint = tie(joint, sent)
    received = []
    for w in range(4):
        others = []
        for g in range(1, half_dp):
            part = chosen(w, near[g], grads_late[w, "near", g])
            part = (part + arrived[w][g].astype(F32)).astype(BF)
            joint = tie(joint, part)
            others.append(to_group(part, g))
        received.append(others)
    mine = []
    for w in range(4):
        part = chosen(w, near[0], grads_late[w, "near", 0])
        mine.append(part + arrived[w][0].astype(F32))
        joint = tie(joint, mine[-1])

    small = [
        jnp.where(first, functools.reduce(jnp.add, x), functools.reduce(jnp.add, y))
        for x, y in zip(zip(*small_early), zip(*small_late))
    ]
    d_norm, d_bqkv, d_bfc = small
    outb = [
        jnp.sum(jnp.where(first, returning[s], ends[s]).astype(F32), axis=0)
        for s in range(seqs)
    ]
    outb = functools.reduce(jnp.add, outb)
    cut = d_norm.shape[1] // count
    d_norm = d_norm.reshape(4, count, cut).swapaxes(0, 1)
    got = lax.dynamic_index_in_dim(d_norm, lane, 0, keepdims=False)
    for step in range(1, count):
        block = lax.dynamic_index_in_dim(d_norm, (lane + step) % count, 0, keepdims=False)
        route = [(i, (i + step) % count) for i in range(count)]
        got = got + lax.ppermute(block, "tensor", route)
    packed = [got, d_bqkv[None], d_bfc[None], outb[None]]
    packed = [
        x.reshape(x.shape[0], dp_count, -1).swapaxes(0, 1).reshape(dp_count, -1) for x in packed
    ]
    sizes = [x.shape[1] for x in packed]
    packed = jnp.concatenate(packed, axis=1)
    small = lax.dynamic_index_in_dim(packed, dp, 0, keepdims=True)
    for step in range(1, dp_count):
        block = lax.dynamic_index_in_dim(packed, (dp + step) % dp_count, 0, keepdims=True)
        route = [(i, (i + step) % dp_count) for i in range(dp_count)]
        small = small + lax.ppermute(block, "dp", route)
    edges = [sum(sizes[:i]) for i in range(len(sizes) + 1)]
    g_norm, g_bqkv, g_bfc, g_outb = [
        small[0, edges[i] : edges[i + 1]] for i in range(len(sizes))
    ]
    g_norm = g_norm.reshape(4, -1)

    results, earlier = [], mine
    for s in range(seqs):
        pieces[s][0] = tie(pieces[s][0], earlier)
        block = summed(pieces[s])
        results.append(gather(block))
        earlier = block
    g_proj, g_out, g_fc, g_qkv = [
        functools.reduce(jnp.add, [x.astype(F32) for x in others], part)
        for part, others in zip(mine, received)
    ]
    boundary_out = jnp.concatenate(results, 0).astype(F32)[None]
    return (
        boundary_out,
        g_norm[None, :2],
        g_norm[None, 2:],
        g_qkv[None],
        g_bqkv[None],
        g_out[None],
        g_fc[None],
        g_bfc[None],
        g_proj[None],
        jnp.stack([g_outb, g_outb])[None],
    )


def solution(mesh):
    step = build(mesh)
    return step


def build(mesh):
    return jax.shard_map(
        shards,
        mesh=mesh,
        in_specs=(
            P("section", "dp", None),
            P("dp", None),
            P("section", None, None),
            P("section", None, None),
            P("section", None, "tensor"),
            P("section", "tensor"),
            P("section", "tensor", None),
            P("section", None, "tensor"),
            P("section", "tensor"),
            P("section", "tensor", None),
            P("section", None, None),
        ),
        out_specs=(
            P("section", "dp", None),
            P("section", None, ("tensor", "dp")),
            P("section", None, ("tensor", "dp")),
            P("section", "dp", "tensor"),
            P("section", ("tensor", "dp")),
            P("section", "tensor", "dp"),
            P("section", "dp", "tensor"),
            P("section", ("tensor", "dp")),
            P("section", "tensor", "dp"),
            P("section", None, "dp"),
        ),
        check_vma=False,
    )
```

```python
import functools

import jax
import jax.numpy as jnp
from jax import lax
from jax.experimental import pallas as pl
from jax.experimental.pallas import tpu as pltpu
from jax.sharding import PartitionSpec as P

HD = 256
ROT = 64
LANES = 128
QB = 256
FT = 512
RB = 512
LB = 128
EPS = 1e-05
BF = jnp.bfloat16
F32 = jnp.float32


def dot_f32(left, right, dims):
    return lax.dot_general(left, right, (dims, ((), ())), preferred_element_type=F32)


def dot(left, right):
    return dot_f32(left, right, ((1,), (0,)))


def dot_rt(left, right):
    return dot_f32(left, right, ((1,), (1,)))


def dot_lt(left, right):
    return dot_f32(left, right, ((0,), (0,)))


def rotary_tables(segments):
    seqs, length = segments.shape
    places = jnp.arange(length, dtype=jnp.int32)
    same = segments[:, :, None] == segments[:, None, :]
    earlier = same & (places[:, None] < places[None, :])[None]
    inside = jnp.sum(earlier.astype(F32), axis=1)
    frequency = 10000.0 ** (-jnp.arange(0, ROT, 2, dtype=F32) / ROT)
    angles = frequency[None, :, None] * inside[:, None, :]
    cosine, sine = jnp.cos(angles), jnp.sin(angles)
    none = jnp.zeros_like(sine)
    rest = jnp.zeros((seqs, LANES - ROT, length), F32)
    return tuple(
        jnp.concatenate(parts, axis=1).swapaxes(1, 2)
        for parts in (
            (cosine, cosine, rest + 1.0),
            (-sine, none, rest),
            (none, sine, rest),
        )
    )


def spin(values, keep, from_right, from_left):
    low, high = values[:, :LANES], values[:, LANES:]
    half = ROT // 2
    turned = (
        low * keep
        + pltpu.roll(low, LANES - half, 1) * from_right
        + pltpu.roll(low, half, 1) * from_left
    )
    return jnp.concatenate([turned, high], axis=1)


def spin_back(grads, keep, from_right, from_left):
    low, high = grads[:, :LANES], grads[:, LANES:]
    half = ROT // 2
    turned = (
        low * keep
        + pltpu.roll(low * from_right, half, 1)
        + pltpu.roll(low * from_left, LANES - half, 1)
    )
    return jnp.concatenate([turned, high], axis=1)


def block_scores(q, k, seg_col, seg_row, at, upto):
    raw = dot_rt(q, k) * HD ** (-0.5)
    rows = lax.broadcasted_iota(jnp.int32, raw.shape, 0) + at
    columns = lax.broadcasted_iota(jnp.int32, raw.shape, 1)
    allowed = (seg_col[at:upto] == seg_row[:, :upto]) & (rows >= columns)
    return jnp.where(allowed, raw, -1e30)


def row_stats(values):
    center = values - jnp.mean(values, axis=-1, keepdims=True)
    spread = jnp.mean(center * center, axis=-1, keepdims=True)
    inverse = lax.rsqrt(spread + EPS)
    return center * inverse, inverse


def row_blocks(length):
    return [(at, min(at + RB, length)) for at in range(0, length, RB)]


def forward_kernel(heads, count, with_pulled, fresh, *refs):
    (
        lane, rows, gains, shifts, w_qkv, b_qkv, keep, from_right, from_left, seg_col, seg_row,
        w_out, w_fc, b_fc, w_proj, added,
    ) = refs[:16]
    refs = refs[16:]
    if with_pulled:
        pulled, refs = refs[0], refs[1:]
    if not fresh:
        refs = refs[5:]
    n1, n2, o_out, a_out, side_out, q_out, k_out, v_out, lse_out = refs[:9]
    pieces, total = refs[9:-1], refs[-1]
    step = pl.program_id(0)
    length = rows.shape[0]

    @pl.when(step == 0)
    def _():
        for at in range(0, length, LB):
            to = at + LB
            hat, _ = row_stats(rows[at:to, :].astype(F32))
            n1[at:to, :] = (hat * gains[0:1, :] + shifts[0:1, :]).astype(BF)
            n2[at:to, :] = (hat * gains[1:2, :] + shifts[1:2, :]).astype(BF)

    @pl.when(step < heads)
    def _():
        tables = (keep[...], from_right[...], from_left[...])
        mixed = dot(n1[...], w_qkv[...]) + b_qkv[...]
        q_out[...] = spin(mixed[:, :HD], *tables).astype(BF)
        k_out[...] = spin(mixed[:, HD : 2 * HD], *tables).astype(BF)
        v_out[...] = mixed[:, 2 * HD :].astype(BF)
        for at in range(0, length, QB):
            upto = at + QB
            scores = block_scores(
                q_out[at:upto, :], k_out[:upto, :], seg_col, seg_row, at, upto
            )
            peak = jnp.max(scores, axis=-1, keepdims=True)
            raised = jnp.exp(scores - peak)
            weight = jnp.sum(raised, axis=-1, keepdims=True)
            probs = (raised / weight).astype(BF)
            o_out[at:upto, :] = dot(probs, v_out[:upto, :]).astype(BF)
            lse_out[0, at:upto, :] = peak + jnp.log(weight)
        part = dot(o_out[...], w_out[...])

        @pl.when(step == 0)
        def _():
            total[...] = part

        @pl.when(step > 0)
        def _():
            total[...] += part

    @pl.when(step >= heads)
    def _():
        for at, to in row_blocks(length):
            u = dot(n2[at:to, :], w_fc[...]) + b_fc[...]
            half_erf = 0.5 * (1.0 + lax.erf(u * 0.7071067811865476))
            a = (u * half_erf).astype(BF)
            slope = half_erf + u * jnp.exp(-0.5 * u * u) * 0.3989422804014327
            if with_pulled:
                slope = slope * pulled[at:to, :].astype(F32)
            a_out[at:to, :] = a
            side_out[at:to, :] = slope.astype(BF)
            total[at:to, :] += dot(a, w_proj[...])

    @pl.when(step == pl.num_programs(0) - 1)
    def _():
        size = length // count
        for d in range(count):
            at = pl.multiple_of(lax.rem(lane[0] + d, count) * size, size)
            part = total[pl.ds(at, size), :]
            if d == 0:
                part = part + rows[pl.ds(at, size), :].astype(F32) + added[...]
            pieces[d][...] = part.astype(BF)


def fixed(shape, *lead):
    block = (None,) * (len(lead) - 1) + tuple(shape) if len(lead) > 1 else tuple(shape)
    index = tuple(lead) + (0,) * (len(block) - len(lead))
    return pl.BlockSpec(block, lambda i: index)


def forward_pass(rows, s, scalars, tables, seg_col, seg_row, weights, added, pulled, joint):
    gains, shifts, w_qkv, b_qkv, w_out, w_fc, b_fc, w_proj = weights
    rows, at = rows
    _, length, width = rows.shape
    seqs = seg_col.shape[0]
    lane, count = scalars
    heads = w_out.shape[0] // HD
    hidden = w_fc.shape[1]
    tiles = hidden // FT
    head = lambda i: jnp.minimum(i, heads - 1)
    tile = lambda i: jnp.maximum(i - heads, 0)
    by_head = lambda r, c, s=0: pl.BlockSpec((r, c), lambda i: (s, head(i)))
    by_tile = lambda r, c, s=0: pl.BlockSpec((r, c), lambda i: (s, tile(i)))
    shape = jax.ShapeDtypeStruct
    block = length // count
    operands = [
        lane, rows, gains, shifts, w_qkv, b_qkv[None], *tables, seg_col, seg_row, w_out, w_fc,
        b_fc[None], w_proj, added[None],
    ]
    in_specs = [
        pl.BlockSpec(memory_space=pltpu.SMEM),
        fixed((length, width), at, 0),
        fixed((2, width)),
        fixed((2, width)),
        by_head(width, 3 * HD),
        by_head(1, 3 * HD),
        *[fixed((length, LANES), s, 0)] * 3,
        fixed((length, 1), s, 0),
        fixed((1, length), s, 0),
        pl.BlockSpec((HD, width), lambda i: (head(i), 0)),
        by_tile(width, FT),
        by_tile(1, FT),
        pl.BlockSpec((FT, width), lambda i: (tile(i), 0)),
        fixed((1, width)),
    ]
    if pulled is not None:
        operands.append(pulled)
        in_specs.append(by_tile(length, FT, s))
    aliases = {}
    if joint is not None:
        aliases = {len(operands) + i: i for i in range(5)}
        operands += joint
        in_specs += [pl.BlockSpec(memory_space=pl.ANY)] * 5
    flops = 2 * length * width * (4 * heads * HD + 2 * hidden)
    rows_all = seqs * length
    result = pl.pallas_call(
        functools.partial(forward_kernel, heads, count, pulled is not None, joint is None),
        grid=(heads + tiles,),
        in_specs=in_specs,
        out_specs=[
            fixed((length, width), s),
            fixed((length, width), s),
            by_head(length, HD, s),
            by_tile(length, FT, s),
            by_tile(length, FT, s),
            *[by_head(length, HD)] * 3,
            pl.BlockSpec((1, length, 1), lambda i: (head(i), 0, 0)),
            *[fixed((block, width))] * count,
        ],
        out_shape=[
            shape((rows_all, width), BF),
            shape((rows_all, width), BF),
            shape((rows_all, heads * HD), BF),
            shape((rows_all, hidden), BF),
            shape((rows_all, hidden), BF),
            *[shape((length, heads * HD), BF)] * 3,
            shape((heads, length, 1), F32),
            *[shape((block, width), BF)] * count,
        ],
        scratch_shapes=[pltpu.VMEM((length, width), F32)],
        input_output_aliases=aliases,
        cost_estimate=pl.CostEstimate(
            flops=flops, bytes_accessed=2 * width * (4 * heads * HD + 2 * hidden), transcendentals=0
        ),
        compiler_params=pltpu.CompilerParams(vmem_limit_bytes=60 << 20),
    )(*operands)
    return result[:5], ((rows, at), *result[5:9]), result[9:]


def backward_kernel(heads, count, ready, fresh, *refs):
    (
        lane, rows, gains, q, k, v, lse, keep, from_right, from_left, seg_col, seg_row, w_qkv,
        side, w_fc,
    ) = refs[:15]
    refs = refs[15:]
    if ready:
        (d_o, own_dy), refs = refs[:2], refs[2:]
    else:
        (flag, dyb, w_out, w_proj), refs = refs[:4], refs[4:]
        late, refs = refs[:count], refs[count:]
    if not fresh:
        refs = refs[1 if ready else 2 :]
    d_mixed, refs = refs[0], refs[1:]
    if not ready:
        d_u, refs = refs[0], refs[1:]
    sums, d_bqkv, d_bfc = refs[:3]
    pieces = refs[3 : 3 + count]
    one, two, dk_acc, dv_acc = refs[3 + count :]
    step = pl.program_id(0)
    length = rows.shape[0]
    scale = HD ** (-0.5)

    @pl.when(step < heads)
    def _():
        tables = (keep[...], from_right[...], from_left[...])
        total_q = jnp.zeros((1, HD), F32)
        out = d_o[...] if ready else dot_rt(dyb[...], w_out[...]).astype(BF)
        for at in reversed(range(0, length, QB)):
            upto = at + QB
            q_now, d_now = q[at:upto, :], out[at:upto]
            scores = block_scores(q_now, k[:upto, :], seg_col, seg_row, at, upto)
            probs = jnp.exp(scores - lse[0, at:upto, :])
            d_probs = dot_rt(d_now, v[:upto, :])
            row = jnp.sum(probs * d_probs, axis=-1, keepdims=True)
            d_scores = (probs * (d_probs - row)).astype(BF)
            dq = dot(d_scores, k[:upto, :]) * scale
            dq = spin_back(dq, *(t[at:upto] for t in tables)).astype(BF)
            d_mixed[at:upto, :HD] = dq
            total_q += jnp.sum(dq.astype(F32), axis=0, keepdims=True)
            if upto == length:
                dk_acc[...] = dot_lt(d_scores, q_now)
                dv_acc[...] = dot_lt(probs.astype(BF), d_now)
            else:
                dk_acc[:upto, :] += dot_lt(d_scores, q_now)
                dv_acc[:upto, :] += dot_lt(probs.astype(BF), d_now)
        dk = spin_back(dk_acc[...] * scale, *tables).astype(BF)
        d_mixed[:, HD : 2 * HD] = dk
        dv = dv_acc[...].astype(BF)
        d_mixed[:, 2 * HD :] = dv
        d_bqkv[:, :HD] = total_q
        d_bqkv[:, HD : 2 * HD] = jnp.sum(dk.astype(F32), axis=0, keepdims=True)
        d_bqkv[:, 2 * HD :] = jnp.sum(dv.astype(F32), axis=0, keepdims=True)
        part = dot_rt(d_mixed[...], w_qkv[...])

        @pl.when(step == 0)
        def _():
            one[...] = part

        @pl.when(step > 0)
        def _():
            one[...] += part

    def tile_step(start):
        bias = jnp.zeros(d_bfc.shape, F32)
        for at, to in row_blocks(length):
            if ready:
                d_now = side[at:to, :]
            else:
                d_now = dot_rt(dyb[at:to, :], w_proj[...]) * side[at:to, :].astype(F32)
                d_now = d_now.astype(BF)
                d_u[at:to, :] = d_now
            bias += jnp.sum(d_now.astype(F32), axis=0, keepdims=True)
            part = dot_rt(d_now, w_fc[...])
            if start:
                two[at:to, :] = part
            else:
                two[at:to, :] += part
        d_bfc[...] = bias

    pl.when(step == heads)(lambda: tile_step(True))
    pl.when(step > heads)(lambda: tile_step(False))

    @pl.when(step == pl.num_programs(0) - 1)
    def _():
        found = [jnp.zeros((1, rows.shape[1]), F32) for _ in range(4)]
        size = length // count
        for d in range(count):
            at = pl.multiple_of(lax.rem(lane[0] + d, count) * size, size)
            now = pl.ds(at, size)
            hat, inverse = row_stats(rows[now, :].astype(F32))
            first, second = one[now, :], two[now, :]
            for i, term in enumerate((first * hat, second * hat, first, second)):
                found[i] += jnp.sum(term, axis=0, keepdims=True)
            both = first * gains[0:1, :] + second * gains[1:2, :]
            both = (
                both
                - jnp.mean(both, axis=-1, keepdims=True)
                - hat * jnp.mean(both * hat, axis=-1, keepdims=True)
            ) * inverse
            if d == 0:
                both = both + (own_dy[...] if ready else dyb[now, :]).astype(F32)
            both = both.astype(BF)
            if not ready:
                both = jnp.where(flag[0] == 0, both, late[d][...])
            pieces[d][...] = both
        for i in range(4):
            sums[i : i + 1, :] = found[i]


def backward_pass(kept, side, s, scalars, tables, seg_col, seg_row, weights, ready, late, joint):
    gains, _, w_qkv, _, w_out, w_fc, _, w_proj = weights
    (rows, row_at), q, k, v, lse = kept
    _, length, width = rows.shape
    lane, count = scalars
    seqs = seg_col.shape[0]
    heads = w_out.shape[0] // HD
    hidden = w_fc.shape[1]
    tiles = hidden // FT
    head = lambda i: jnp.minimum(i, heads - 1)
    tile = lambda i: jnp.maximum(i - heads, 0)
    by_head = lambda r, c, s=0: pl.BlockSpec((r, c), lambda i: (s, head(i)))
    by_tile = lambda r, c, s=0: pl.BlockSpec((r, c), lambda i: (s, tile(i)))
    shape = jax.ShapeDtypeStruct
    block = length // count
    smem = pl.BlockSpec(memory_space=pltpu.SMEM)
    operands = [lane, rows, gains, q, k, v, lse, *tables, seg_col, seg_row, w_qkv, side, w_fc]
    in_specs = [
        smem,
        fixed((length, width), row_at, 0),
        fixed((2, width)),
        *[by_head(length, HD)] * 3,
        pl.BlockSpec((1, length, 1), lambda i: (head(i), 0, 0)),
        *[fixed((length, LANES), s, 0)] * 3,
        fixed((length, 1), s, 0),
        fixed((1, length), s, 0),
        by_head(width, 3 * HD),
        by_tile(length, FT, s),
        by_tile(width, FT),
    ]
    rows_all = seqs * length
    out_specs = [by_head(length, 3 * HD, s)]
    out_shape = [shape((rows_all, 3 * heads * HD), BF)]
    if ready is not None:
        operands += list(ready)
        in_specs += [by_head(length, HD, s), fixed((block, width))]
    else:
        flag, dyb, others = late
        operands += [flag, dyb, w_out, w_proj, *others]
        in_specs += [
            smem,
            fixed((length, width)),
            pl.BlockSpec((HD, width), lambda i: (head(i), 0)),
            pl.BlockSpec((FT, width), lambda i: (tile(i), 0)),
            *[fixed((block, width))] * count,
        ]
        out_specs.append(by_tile(length, FT, s))
        out_shape.append(shape((rows_all, hidden), BF))
    aliases = {}
    if joint is not None:
        aliases = {len(operands) + i: i for i in range(len(joint))}
        operands += joint
        in_specs += [pl.BlockSpec(memory_space=pl.ANY)] * len(joint)
    n_joint = len(out_specs)
    out_specs += [fixed((4, width)), by_head(1, 3 * HD), by_tile(1, FT)]
    out_specs += [fixed((block, width))] * count
    out_shape += [
        shape((4, width), F32),
        shape((1, 3 * heads * HD), F32),
        shape((1, hidden), F32),
        *[shape((block, width), BF)] * count,
    ]
    flops = 2 * length * width * (3 * heads * HD + hidden) * (1 if ready is not None else 2)
    result = pl.pallas_call(
        functools.partial(backward_kernel, heads, count, ready is not None, joint is None),
        grid=(heads + tiles,),
        in_specs=in_specs,
        out_specs=out_specs,
        out_shape=out_shape,
        scratch_shapes=[pltpu.VMEM((length, width), F32)] * 2
        + [pltpu.VMEM((length, HD), F32)] * 2,
        input_output_aliases=aliases,
        cost_estimate=pl.CostEstimate(
            flops=flops, bytes_accessed=2 * width * (3 * heads * HD + hidden), transcendentals=0
        ),
        compiler_params=pltpu.CompilerParams(vmem_limit_bytes=60 << 20),
    )(*operands)
    joint, rest = result[:n_joint], result[n_joint:]
    sums, d_bqkv, d_bfc = rest[:3]
    return joint, (sums, d_bqkv[0], d_bfc[0]), rest[3:]


def tie(values, *earlier):
    return lax.optimization_barrier((values, earlier))[0]


def shards(
    boundary_in,
    segment_ids,
    norm_gains,
    norm_biases,
    w_qkv,
    b_qkv,
    w_out,
    w_fc,
    b_fc,
    w_proj,
    out_biases,
):
    w_qkv, w_out, w_fc, w_proj = w_qkv[0], w_out[0], w_fc[0], w_proj[0]
    b_qkv, b_fc = b_qkv[0].astype(F32), b_fc[0].astype(F32)
    gains, shifts = norm_gains[0].astype(F32), norm_biases[0].astype(F32)
    added = out_biases[0, 0].astype(F32) + out_biases[0, 1].astype(F32)
    weights = (gains, shifts, w_qkv, b_qkv, w_out, w_fc, b_fc, w_proj)
    seqs, length = segment_ids.shape
    flat = boundary_in[0]
    ends = flat.reshape(seqs, length, -1)
    section = lax.axis_index("section")
    lane = lax.axis_index("tensor")
    count = lax.axis_size("tensor")
    first = section == 0
    dp = lax.axis_index("dp")
    dp_count = lax.axis_size("dp")
    scalars = (lane[None], count)
    tables = rotary_tables(segment_ids)
    columns, lines = segment_ids[:, :, None], segment_ids[:, None, :]

    def own(values, at=0):
        size = length // count
        return lax.dynamic_slice_in_dim(values, at * length + lane * size, size, 0)

    def ring(step, origin, target):
        return [(origin * count + i, target * count + (i + step) % count) for i in range(count)]

    both = ("section", "tensor")

    def scatter(blocks, origin):
        pieces = []
        for step, block in enumerate(blocks):
            pieces.append(lax.ppermute(block, both, ring(step, origin, 1 - origin)))
        return pieces

    def scatter_within(blocks):
        pieces = [blocks[0]]
        for step in range(1, count):
            route = [(i, (i + step) % count) for i in range(count)]
            pieces.append(lax.ppermute(blocks[step], "tensor", route))
        return pieces

    def summed(pieces):
        return functools.reduce(jnp.add, [p.astype(F32) for p in pieces]).astype(BF)

    def gather(block, where=None):
        size = block.shape[0]
        whole = jnp.zeros((count * size,) + block.shape[1:], block.dtype)
        for step in range(count):
            piece = block
            if step:
                if where is None:
                    route = [(i, (i + step) % count) for i in range(count)]
                    piece = lax.ppermute(block, "tensor", route)
                else:
                    piece = lax.ppermute(block, both, ring(step, where, where))
            whole = lax.dynamic_update_slice_in_dim(
                whole, piece, ((lane - step) % count) * size, 0
            )
        return whole

    def forward(rows, s, joint, pulled=None):
        return forward_pass(rows, s, scalars, tables, columns, lines, weights, added, pulled, joint)

    def backward(kept, side, s, joint, ready=None, late=None):
        return backward_pass(
            kept, side, s, scalars, tables, columns, lines, weights, ready, late, joint
        )

    early, pieces, joint, before = [], [], None, None
    for s in range(seqs):
        rows = ends if s == 0 else tie(ends, before)
        joint, kept, before = forward((rows, s), s, joint)
        early.append(((ends, s), *kept[1:]))
        pieces.append(scatter(before, 0))
    joint_early = joint
    blocks = []
    for s in range(seqs):
        if s == 1:
            pulled = dot_rt(tie(flat, blocks[0]), w_proj).astype(BF)
            d_o = dot_rt(tie(flat, pulled), w_out).astype(BF)
            before = (pulled, d_o)
        pieces[s][0] = tie(pieces[s][0], before, *blocks)
        blocks.append(summed(pieces[s]))
    inputs = [gather(block, 1) for block in blocks]
    inputs[0] = tie(inputs[0], blocks[-1])

    late_out, small_late, pieces = [], [], []
    joint, joint_back, before = None, None, None
    for s in range(seqs):
        rows = inputs[s] if s == 0 else tie(inputs[s], before)
        joint, kept, out = forward((rows[None], 0), s, joint, pulled)
        late_out.append(out)
        ready = (d_o, own(flat, s))
        joint_back, small, before = backward(kept, joint[4], s, joint_back, ready)
        small_late.append(small)
        pieces.append(scatter(before, 1))
    n1, n2, o, a, d_u = joint
    (d_mixed,) = joint_back
    pieces[0][0] = tie(pieces[0][0], before)
    blocks = [summed(pieces[0])]
    pairs = [(a, flat), (o, flat), (n2, d_u), (n1, d_mixed)]
    whole_late, before = [], blocks[0]
    for w, (left, right) in enumerate(pairs):
        if w == 3:
            for s in range(1, seqs):
                pieces[s][0] = tie(pieces[s][0], before, *blocks)
                blocks.append(summed(pieces[s]))
            before = blocks[-1]
        before = dot_lt(tie(left, before), right).astype(BF)
        whole_late.append(before)
    returning = [gather(block, 0) for block in blocks]

    half_dp = dp_count // 2
    group, core = dp // 2, dp % 2
    away = [((group + g) % half_dp) * 2 + 1 - core for g in range(half_dp)]
    near = [((group + g) % half_dp) * 2 + core for g in range(half_dp)]
    n1, n2, o, a, slope = joint_early
    arrived, others, mine = {}, {}, {}

    def part_of(w, block, left, right, before):
        cut_left = w >= 2
        cut = left if cut_left else right
        size = cut.shape[1] // dp_count
        left, right = tie((left, right), before)
        cut = lax.dynamic_slice_in_dim(left if cut_left else right, block * size, size, 1)
        early = dot_lt(cut, right) if cut_left else dot_lt(left, cut)
        kept = lax.dynamic_slice_in_dim(
            whole_late[w], block * size, size, 0 if cut_left else 1
        )
        return jnp.where(first, early, kept.astype(F32))

    def leave(pairs, groups, before):
        for w, left, right in pairs:
            for g in groups:
                before = part_of(w, away[g], left, right, before).astype(BF)
                arrived[w, g] = lax.ppermute(before, "dp", [(i, i ^ 1) for i in range(dp_count)])
        return before

    def pass_on(pairs, before):
        for w, left, right in pairs:
            for g in range(1, half_dp):
                part = part_of(w, near[g], left, right, before)
                before = (part + arrived[w, g].astype(F32)).astype(BF)
                route = [(i, (i + 2 * g) % dp_count) for i in range(dp_count)]
                others.setdefault(w, []).append(lax.ppermute(before, "dp", route))
        return before

    small_early, pieces, joint_back = [], [], None
    for s in range(seqs):
        dyb = tie(returning[s], before)
        if s == seqs - 1:
            dy_all = jnp.concatenate(returning[:-1] + [dyb], 0)
            ends_pairs = [(0, a, dy_all), (1, o, dy_all)]
            before = leave(ends_pairs, range(1, half_dp), before)
            before = pass_on(ends_pairs, before)
            dyb = tie(dyb, before)
        flag = section[None]
        joint_back, small, before = backward(
            early[s], slope, s, joint_back, late=(flag, dyb, late_out[s])
        )
        small_early.append(small)
        pieces.append(scatter_within(before))
    d_mixed, d_u = joint_back
    inner_pairs = [(2, n2, d_u), (3, n1, d_mixed)]

    results, blocks = [], []
    for s in range(seqs - 1):
        pieces[s][0] = tie(pieces[s][0], before)
        blocks.append(summed(pieces[s]))
    before = (before, blocks)
    before = leave(inner_pairs, range(1, half_dp), before)
    before = pass_on(inner_pairs, before)
    small = [
        jnp.where(first, functools.reduce(jnp.add, x), functools.reduce(jnp.add, y))
        for x, y in zip(zip(*small_early), zip(*small_late))
    ]
    d_norm, d_bqkv, d_bfc = small
    d_outb = jnp.sum(jnp.where(first, dy_all, flat).astype(F32), axis=0)
    packed = [
        x.reshape(x.shape[0] * parts, dp_count, -1).swapaxes(0, 1).reshape(dp_count, -1)
        for x, parts in ((d_norm, count), (d_bqkv[None], 1), (d_bfc[None], 1), (d_outb[None], 1))
    ]
    sizes = [x.shape[1] for x in packed]
    packed = jnp.concatenate(packed, axis=1)
    packed = tie(packed, before)
    parts = [lax.dynamic_index_in_dim(packed, dp, 0, keepdims=True)]
    for step in range(1, dp_count):
        block = lax.dynamic_index_in_dim(packed, (dp + step) % dp_count, 0, keepdims=True)
        route = [(i, (i + step) % dp_count) for i in range(dp_count)]
        parts.append(lax.ppermute(block, "dp", route))
    pieces[-1][0] = tie(pieces[-1][0], before)
    blocks.append(summed(pieces[-1]))
    results = [gather(block) for block in blocks]
    pairs = ends_pairs + inner_pairs
    before = leave(pairs, [0], (before, blocks))
    for w, left, right in pairs:
        before = part_of(w, near[0], left, right, before)
        mine[w] = before + arrived[w, 0].astype(F32)
    parts[0] = tie(parts[0], mine)
    total = functools.reduce(jnp.add, parts)
    edges = [sum(sizes[:i]) for i in range(len(sizes) + 1)]
    norm, g_bqkv, g_bfc, g_outb = [total[0, edges[i] : edges[i + 1]] for i in range(len(sizes))]
    norm = norm.reshape(4, count, -1).swapaxes(0, 1)
    g_norm = lax.dynamic_index_in_dim(norm, lane, 0, keepdims=False)
    for step in range(1, count):
        block = lax.dynamic_index_in_dim(norm, (lane + step) % count, 0, keepdims=False)
        route = [(i, (i + step) % count) for i in range(count)]
        g_norm = g_norm + lax.ppermute(block, "tensor", route)

    g_proj, g_out, g_fc, g_qkv = [
        functools.reduce(jnp.add, [x.astype(F32) for x in others[w]], mine[w]) for w in range(4)
    ]
    boundary_out = jnp.concatenate(results, 0).astype(F32)[None]
    return (
        boundary_out,
        g_norm[None, :2],
        g_norm[None, 2:],
        g_qkv[None],
        g_bqkv[None],
        g_out[None],
        g_fc[None],
        g_bfc[None],
        g_proj[None],
        jnp.stack([g_outb, g_outb])[None],
    )


def solution(mesh):
    step = build(mesh)
    return step


def build(mesh):
    return jax.shard_map(
        shards,
        mesh=mesh,
        in_specs=(
            P("section", "dp", None),
            P("dp", None),
            P("section", None, None),
            P("section", None, None),
            P("section", None, "tensor"),
            P("section", "tensor"),
            P("section", "tensor", None),
            P("section", None, "tensor"),
            P("section", "tensor"),
            P("section", "tensor", None),
            P("section", None, None),
        ),
        out_specs=(
            P("section", "dp", None),
            P("section", None, ("tensor", "dp")),
            P("section", None, ("tensor", "dp")),
            P("section", "dp", "tensor"),
            P("section", ("tensor", "dp")),
            P("section", "tensor", "dp"),
            P("section", "dp", "tensor"),
            P("section", ("tensor", "dp")),
            P("section", "tensor", "dp"),
            P("section", None, "dp"),
        ),
        check_vma=False,
    )
```
